256 devices in a mesh: req: 16 (over x, y), seq: 16 (over z, core).
Axes of the slice: x: 4, y: 4, z: 8, core: 2. Of those that a mesh axis runs over, the one named last changes fastest.
Arguments:
- store: bfloat16 [144, 16, 56, 1024], P('req', 'seq'), may hold values from -6 to 6
- passage_owner: int32 [16, 256, 1], P(None, 'seq'), may hold values from 0 to 15; in each aligned block of 16 rows (0 to 15, 16 to 31, ..., all dimensions but the last counted through in order) at most 2 rows name the same one
- passage_slot: int32 [16, 256], P(None, 'seq'), may hold values from 0 to 8
- sel_pos: int32 [16, 1792], P('req'), may hold values from 0 to 14335, as said below
- queries: bfloat16 [16, 1792, 2048], P('req', 'seq'), may hold values from -512 to 512
- new_kv: bfloat16 [16, 1792, 1024], P('req', 'seq'), may hold values from -6 to 6
Outputs:
- blended_kv: bfloat16 [16, 14336, 1024], P('req', 'seq')
- deviation: float32 [16, 1792, 4], P('req', 'seq')
- attended: bfloat16 [16, 1792, 2048], P('req', 'seq')
The draws below stay inside these ranges and needn't reach their ends.
Inputs may be any that keep to these rules, and one draw needn't show every extreme that they name: `passage_owner`: within the 16 pieces of one request's position block no owner is named more than 2 times, and some block names one owner exactly 2 times. `sel_pos`: entries b * 112 to (b + 1) * 112 - 1 of a request are distinct positions of block b, between b * 896 and (b + 1) * 896 - 1.
All inputs are finite; a program needn't handle non-finite values.
Results may differ from the reference program's by a relative error of at most 0.005.
Values may be sent and summed in bfloat16 or wider, within the bound.
A program may use at most 128 MiB of HBM per device.

```python
import math
import jax
import jax.numpy as jnp
import numpy as np
from jax import lax

HEAD_DIM = 128
KV_HEADS = 4
PASSAGE = 56
PASSAGES_DEV = 16
STORE_DEV = 9
SLOT_CAP = 2
TOK_DEV = 896
SEL_DEV = 112
REQUESTS = 16
SEQ_BLOCKS = 16
LENGTH = 14336
SELECTED = 1792
PASSAGES_REQ = 256
STORE_ROWS = 144
Q_WIDTH = 2048
KV_WIDTH = 1024
GROUP = 4
N_REQ = 16


def drawn_parts(key):
    base_kv = jax.random.normal(jax.random.fold_in(key, 101), (REQUESTS, SELECTED, KV_WIDTH), jnp.float32)
    base_kv = jnp.clip(base_kv, -6.0, 6.0)
    return base_kv


def draw_new_kv(key, part):
    base_kv = drawn_parts(key)
    return base_kv.astype(jnp.bfloat16)


def draw_queries(key, part):
    drawn_rows = jax.random.normal(jax.random.fold_in(key, 303), (REQUESTS, SELECTED, Q_WIDTH), jnp.float32)
    return jnp.clip(drawn_rows, -6.0, 6.0).astype(jnp.bfloat16)


def draw_sel_pos(key, part):
    block_keys = jax.random.split(jax.random.fold_in(key, 404), REQUESTS * SEQ_BLOCKS)
    offsets = jax.vmap(lambda block_key: jax.random.permutation(block_key, TOK_DEV)[:SEL_DEV])(block_keys)
    block_start = jnp.arange(REQUESTS * SEQ_BLOCKS, dtype=jnp.int32) % SEQ_BLOCKS * TOK_DEV
    positions = offsets.astype(jnp.int32) + block_start[:, None]
    return positions.reshape(REQUESTS, SELECTED)


def set_ends(drawn, rng, smallest, largest):
    extent = drawn.shape
    index_at = [jax.random.randint(jax.random.fold_in(rng, axis), (), 0, extent[axis]) for axis in range(len(extent))]
    drawn = drawn.at[tuple(index_at)].set(smallest)
    longest = extent.index(max(extent))
    index_at[longest] = (index_at[longest] + 1) % extent[longest]
    return drawn.at[tuple(index_at)].set(largest)


def block_scale(rng, shape, shards, smallest, largest):
    level, own = 1.0, jax.random.fold_in(rng, 6)
    for position, blocks in shards:
        steps = jnp.exp(jax.random.uniform(jax.random.fold_in(own, position), (blocks,), jnp.float32, smallest / len(shards), largest / len(shards)))
        level = level * jnp.repeat(steps, shape[position] // blocks).reshape([-1 if axis == position else 1 for axis in range(len(shape))])
    return level


def routed_block(rng, own, number, rows, amount, top, bound, skew):
    sequence = jax.random.permutation(rng, amount)
    packed, usual = portions_of(amount, rows * top, bound, skew, True), portions_of(amount, rows * top, bound, skew, False)
    places = jnp.arange(amount)

    def named(tallies, offset_by):
        used = int((tallies > 0).sum())
        fixed = max(1, used // 4)
        passed = fixed + (places - fixed + offset_by * (used - fixed)) % max(1, amount - fixed)
        return jnp.zeros((amount,), jnp.int32).at[sequence[jnp.where(places < fixed, places, passed)]].set(jnp.asarray(tallies, jnp.int32))

    tallies = jnp.where(number % 4 == 0, named(packed, number // 4), named(usual, number - number // 4 - 1))
    mixed = jax.random.permutation(jax.random.fold_in(own, 3), amount)
    source_of, taker = mixed[0:amount // 2 * 2:2], mixed[1:amount // 2 * 2:2]
    room = jnp.minimum(tallies[source_of] - 1, bound - tallies[taker]) // 2
    room = jnp.where((source_of == sequence[0]) | (taker == sequence[0]) | (tallies[taker] == 0), 0, jnp.maximum(room, 0))
    passed = jax.random.randint(jax.random.fold_in(own, 4), (amount // 2,), 0, 1 << 20) % (room + 1)
    tallies = tallies.at[source_of].add(-passed).at[taker].add(passed)
    items = jnp.searchsorted(jnp.cumsum(tallies), jnp.arange(rows * top), side="right").astype(jnp.int32)
    grid = items.reshape(top, rows).T
    grid = grid[jax.random.permutation(jax.random.fold_in(own, 1), rows)]
    offset_by = jax.random.randint(jax.random.fold_in(own, 2), (rows, 1), 0, top)
    return jnp.take_along_axis(grid, (jnp.arange(top)[None, :] + offset_by) % top, axis=1)


def portions_of(count, total, bound, skew, full):
    weights = [(1 << 20) // math.isqrt(standing ** skew) + 1 for standing in range(1, count + 1)]
    largest = bound if full else min(bound, max(-(-total // count), total * weights[0] // sum(weights)))
    least = 1 if total - largest >= count - 1 else 0
    holding, rest = [largest] + [least] * (count - 1), total - largest - least * (count - 1)
    while rest > 0:
        free = [i for i in range(1, count) if holding[i] < largest] or [i for i in range(1, count) if holding[i] < bound]
        pool, remaining = sum([weights[i] for i in free]), rest
        for i in free:
            extra = min(bound - holding[i], max(1, remaining * weights[i] // pool), rest)
            holding[i] = holding[i] + extra
            rest = rest - extra
    return np.array(holding)


def scatter_about(stream_key, dims, width, most, pieces=(), kind=jnp.bfloat16):
    factor_of = block_scale(stream_key, dims, pieces, -0.22, 0.18) if pieces else 1.0
    values = jax.random.normal(stream_key, dims, jnp.float32) * width * factor_of
    return jnp.minimum(jnp.maximum(values, -most), most).astype(kind)


def setup_inputs(seed: int = 0) -> dict:
    arg_keys = jax.random.split(jax.random.key(seed), 7)
    store = scatter_about(arg_keys[0], (STORE_ROWS, SEQ_BLOCKS, PASSAGE, KV_WIDTH), 1.0, 6.0, ((0, 16), (1, 16)))
    passage_owner_keys = jax.random.split(jax.random.fold_in(arg_keys[1], 1), REQUESTS * PASSAGES_REQ // PASSAGES_DEV)
    passage_owner_turns = jax.random.permutation(jax.random.fold_in(arg_keys[1], 3), REQUESTS * PASSAGES_REQ // PASSAGES_DEV)
    passage_owner = jax.vmap(lambda own, number: routed_block(jax.random.fold_in(arg_keys[1], 2), own, number, PASSAGES_DEV, N_REQ, 1, SLOT_CAP, 2))(passage_owner_keys, passage_owner_turns).reshape((REQUESTS, PASSAGES_REQ, 1))
    passage_slot = set_ends(jax.random.randint(arg_keys[2], (REQUESTS, PASSAGES_REQ), 0, STORE_DEV), jax.random.fold_in(arg_keys[2], 1), 0, STORE_DEV - 1).astype(jnp.int32)
    sel_pos = draw_sel_pos(jax.random.fold_in(arg_keys[6], 71), 0)
    queries = draw_queries(jax.random.fold_in(arg_keys[6], 71), 0)
    new_kv = draw_new_kv(jax.random.fold_in(arg_keys[6], 71), 0)
    return {"store": store, "passage_owner": passage_owner, "passage_slot": passage_slot, "sel_pos": sel_pos, "queries": queries, "new_kv": new_kv}


def attend(query_rows, query_pos, key_value):
    key_count = key_value.shape[0]
    score_scale = HEAD_DIM ** -0.5
    query_full = query_rows.astype(jnp.float32).reshape(SEL_DEV, KV_HEADS, GROUP, HEAD_DIM)
    key_rows = key_value[:, :KV_HEADS * HEAD_DIM].astype(jnp.float32).reshape(key_count, KV_HEADS, HEAD_DIM)
    value_rows = key_value[:, KV_HEADS * HEAD_DIM:].astype(jnp.float32).reshape(key_count, KV_HEADS, HEAD_DIM)
    scores = jnp.einsum('qkgd,pkd->qkgp', query_full, key_rows) * score_scale
    key_pos = jnp.arange(key_count, dtype=jnp.int32)
    visible = key_pos[None, None, None, :] <= query_pos[:, None, None, None]
    scores = jnp.where(visible, scores, -jnp.inf)
    running_max = jnp.max(scores, axis=-1, keepdims=True)
    weights = jnp.exp(scores - running_max)
    weight_sum = jnp.sum(weights, axis=-1)
    rounded = lax.optimization_barrier(weights.astype(jnp.bfloat16)).astype(jnp.float32)
    summed = jnp.einsum('qkgp,pkd->qkgd', rounded, value_rows)
    output_rows = summed / weight_sum[..., None]
    return output_rows.reshape(SEL_DEV, Q_WIDTH).astype(jnp.bfloat16)


def reference(store, passage_owner, passage_slot, sel_pos, queries, new_kv):
    owner_index = passage_owner[:, :, 0].astype(jnp.int32)
    row_index = owner_index * STORE_DEV + passage_slot.astype(jnp.int32)
    column = (jnp.arange(PASSAGES_REQ, dtype=jnp.int32) // PASSAGES_DEV)[None, :]
    cached = store[row_index, column].reshape(REQUESTS, LENGTH, KV_WIDTH)
    request_ids = jnp.arange(REQUESTS, dtype=jnp.int32)[:, None]
    positions = sel_pos.astype(jnp.int32)
    picked = cached[request_ids, positions]
    blended = cached.at[request_ids, positions].set(new_kv)
    difference = new_kv.astype(jnp.float32) - picked.astype(jnp.float32)
    squared = (difference * difference).reshape(REQUESTS, SELECTED, 2, KV_HEADS, HEAD_DIM)
    deviation = jnp.sum(squared, axis=(2, 4))
    pieces_out = []
    for seq_index in range(SEQ_BLOCKS):
        query_block = queries[:, seq_index * SEL_DEV:(seq_index + 1) * SEL_DEV]
        pos_block = positions[:, seq_index * SEL_DEV:(seq_index + 1) * SEL_DEV]
        key_block = blended[:, :(seq_index + 1) * TOK_DEV]
        pieces_out.append(lax.map(lambda items: attend(items[0], items[1], items[2]), (query_block, pos_block, key_block)))
    attended = jnp.concatenate(pieces_out, axis=1)
    return blended, deviation, attended
```

```python
import math

import jax
import jax.numpy as jnp
from jax import lax
from jax.experimental import pallas as pl
from jax.experimental.pallas import tpu as pltpu
from jax.sharding import PartitionSpec as P

NREQ = 16
NZ = 8
PIECES = 16
PASSAGE = 56
TOK = 896
SEL = 112
KVW = 1024
QW = 2048
D = 128
CHIP_TOK = 2 * TOK
C2 = (D ** -0.5) * math.log2(math.e)
EMPTY = -1e30
F32 = jnp.float32
BF16 = jnp.bfloat16
MESH = pl.DeviceIdType.MESH


def remote(src, dst, ssem, rsem, req, seq):
    return pltpu.make_async_remote_copy(
        src_ref=src,
        dst_ref=dst,
        send_sem=ssem,
        recv_sem=rsem,
        device_id=(req, seq),
        device_id_type=MESH,
    )


def kernel(
    owner, slot, pos, store, q, fresh_kv,
    blended_out, dev, att,
    outgoing, incoming, qh, qg, cached, blend, bh, kv, part, lse,
    buf_o, buf_l, fin,
    a_send, a_recv, qx_sem, qs_sem, qr_sem, kx_sem, ps_sem, pr_sem, fx_sem, b_sem,
):
    me = lax.axis_index("req")
    seq = lax.axis_index("seq")
    s = seq // 2
    c = seq % 2
    mate = s * 2 + (1 - c)
    above = lax.rem(s + 1, NZ) * 2 + c
    below = lax.rem(s + NZ - 1, NZ) * 2 + c

    def partner(i):
        return lax.rem(me + i, NREQ)

    barrier = pltpu.get_barrier_semaphore()
    for i in range(1, NREQ):
        pl.semaphore_signal(barrier, inc=1, device_id=(partner(i), seq), device_id_type=MESH)
    for z in (mate, above, below):
        pl.semaphore_signal(barrier, inc=1, device_id=(me, z), device_id_type=MESH)

    def build(r, carry):
        count = jnp.int32(0)
        first = jnp.int32(0)
        second = jnp.int32(0)
        for j in range(PIECES):
            hit = owner[r, j] == me
            value = slot[r, j]
            first = jnp.where(hit & (count == 0), value, first)
            second = jnp.where(hit & (count == 1), value, second)
            count = count + hit.astype(jnp.int32)
        outgoing[r, 0] = store[first]
        outgoing[r, 1] = store[second]
        return carry

    lax.fori_loop(0, NREQ, build, 0)
    for h in range(16):
        qh[h] = q[:, h * D : (h + 1) * D]
    pl.semaphore_wait(barrier, NREQ - 1 + 3)

    def a2a(i):
        return remote(
            outgoing.at[partner(i)], incoming.at[me], a_send.at[i], a_recv.at[i], partner(i), seq
        )

    def a2a_wait(i):
        src = lax.rem(me - i + NREQ, NREQ)
        return remote(
            outgoing.at[src], incoming.at[src], a_send.at[i], a_recv.at[i], src, seq
        )

    qx = remote(qh.at[pl.ds((1 - c) * 8, 8)], qg.at[s, :, c], qx_sem.at[0], qx_sem.at[1], me, mate)
    qx.start()
    order = [4, 12, 1, 3, 5, 13, 7, 15, 8, 2, 9, 6, 11, 14, 10]
    for i in order:
        a2a(i).start()
    incoming[me] = outgoing[me]
    for h in range(8):
        qg[s, h, c] = qh[c * 8 + h]
    remote(qh.at[pl.ds(0, 8)], qg.at[s, :, 1 - c], qx_sem.at[0], qx_sem.at[1], me, mate).wait_recv()

    def q_msg(z, t, up):
        if t == 4:
            ref = qg.at[z, pl.ds(4 if up else 0, 4)]
        else:
            ref = qg.at[z]
        k = 1 if up else 0
        return remote(ref, ref, qs_sem.at[k, t], qr_sem.at[k, t], me, above if up else below)

    for t in range(1, 5):
        z_down = s + t - 1
        z_up = lax.rem(s - t + 1 + NZ, NZ)
        if t > 1:

            @pl.when(z_down <= NZ - 1)
            def _(z=z_down, t=t):
                q_msg(z, t - 1, False).wait_recv()

        @pl.when((z_down <= NZ - 1) & (s >= 1))
        def _(z=z_down, t=t):
            q_msg(z, t, False).start()

        if t > 1:

            @pl.when(z_up >= 4)
            def _(z=z_up, t=t):
                q_msg(z, t - 1, True).wait_recv()

        @pl.when(z_up >= 4)
        def _(z=z_up, t=t):
            q_msg(z, t, True).start()

    eye = lax.broadcasted_iota(jnp.int32, (SEL, D), 0) == lax.broadcasted_iota(jnp.int32, (SEL, D), 1)

    def to_col(row):
        return jnp.sum(jnp.where(eye, row, 0.0), axis=1, keepdims=True)

    def to_row(col):
        return jnp.sum(jnp.where(eye, col, 0.0), axis=0, keepdims=True)

    own_row = pos[0:1, :]
    pick = (lax.broadcasted_iota(jnp.int32, (SEL, TOK), 1).astype(F32) == to_col(own_row)).astype(BF16)
    put = lax.broadcasted_iota(jnp.int32, (TOK, D), 0).astype(F32) == own_row
    hit_col = jnp.sum(jnp.where(put, 1.0, 0.0), axis=1, keepdims=True) > 0.5
    put = jnp.where(put, 1.0, 0.0).astype(BF16)[:, :SEL]

    for i in range(1, NREQ):
        a2a_wait(i).wait_recv()
    mine = [owner[me, j] for j in range(PIECES)]
    for j in range(PIECES):
        rank = jnp.int32(0)
        for k in range(j):
            rank = rank + (mine[k] == mine[j]).astype(jnp.int32)
        cached[j * PASSAGE : (j + 1) * PASSAGE, :] = incoming[mine[j], jnp.minimum(rank, 1)]

    squares = []
    for g in range(8):
        cols = slice(g * D, (g + 1) * D)
        old = cached[:, cols]
        new = fresh_kv[:, cols]
        placed = jnp.dot(put, new, preferred_element_type=F32)
        both = jnp.where(hit_col, placed, old.astype(F32)).astype(BF16)
        blend[:, cols] = both
        bh[g // 4, (g % 4) // 2, g % 2] = both
        picked = jnp.dot(pick, old, preferred_element_type=F32)
        diff = new.astype(F32) - picked
        squares.append(jnp.sum(diff * diff, axis=1, keepdims=True))
    kx = remote(bh.at[:, 1 - c], kv.at[:, :, c], kx_sem.at[0], kx_sem.at[1], me, mate)
    kx.start()
    out_copy = pltpu.make_async_copy(blend, blended_out, b_sem)
    out_copy.start()
    for k in range(2):
        for h in range(2):
            kv[k, h, c] = bh[k, c, h]
    for h in range(4):
        dev[:, h : h + 1] = squares[h] + squares[4 + h]

    @pl.when(s + 4 <= NZ - 1)
    def _():
        q_msg(s + 4, 4, False).wait_recv()

    @pl.when(lax.rem(s + 4, NZ) >= 4)
    def _():
        q_msg(lax.rem(s + 4, NZ), 4, True).wait_recv()

    remote(bh.at[:, c], kv.at[:, :, 1 - c], kx_sem.at[0], kx_sem.at[1], me, mate).wait_recv()

    def attend(zd, masked):
        def half(step, carry):
            kvh = step // 2
            first = kvh * 4 + (step % 2) * 2
            rows = qg[zd, pl.ds(first, 2)].reshape(4 * SEL, D)
            keys = kv[0, kvh].reshape(CHIP_TOK, D)
            values = kv[1, kvh].reshape(CHIP_TOK, D)
            scores = lax.dot_general(
                rows, keys, (((1,), (1,)), ((), ())), preferred_element_type=F32
            )
            if masked:
                limit = [to_col(pos[1:2, :]), to_col(pos[2:3, :])]
                limit = jnp.concatenate(limit + limit, axis=0)
                index = lax.broadcasted_iota(jnp.int32, (4 * SEL, CHIP_TOK), 1).astype(F32)
                scores = jnp.where(index <= limit, scores, EMPTY)
            top = jnp.max(scores, axis=1, keepdims=True)
            weights = jnp.exp2((scores - top) * C2)
            total = jnp.sum(weights, axis=1, keepdims=True)
            product = jnp.dot(weights.astype(BF16), values, preferred_element_type=F32)
            result = (product / total).astype(BF16)
            part[zd, pl.ds(first, 2)] = result.reshape(2, 2, SEL, D)
            level = top * C2 + jnp.log2(total)
            for g in range(4):
                lse[zd, kvh, pl.ds((step % 2) * 4 + g, 1), :] = to_row(level[g * SEL : (g + 1) * SEL])
            return carry

        lax.fori_loop(0, 4, half, 0)

    def merge(zd, kvh, k, slot_at):
        have = lse[zd, kvh]
        came = buf_l[k, slot_at, kvh]
        high = jnp.maximum(have, came)
        e_have = jnp.exp2(have - high)
        e_came = jnp.exp2(came - high)
        total = e_have + e_came
        share = e_came / total
        for g in range(4):
            for b in range(2):
                w = to_col(share[g * 2 + b : g * 2 + b + 1, :])
                x = part[zd, kvh * 4 + g, b].astype(F32)
                y = buf_o[k, slot_at, kvh * 4 + g, b].astype(F32)
                part[zd, kvh * 4 + g, b] = (x + w * (y - x)).astype(BF16)
        lse[zd, kvh] = high + jnp.log2(total)

    def p_msgs(zd, d, k, peer, half):
        if half is None:
            o_src, o_dst = part.at[zd], buf_o.at[k, d - 1]
        else:
            o_src = part.at[zd, pl.ds(half * 4, 4)]
            o_dst = buf_o.at[k, d - 1, pl.ds(half * 4, 4)]
        return (
            remote(o_src, o_dst, ps_sem.at[k, d, 0], pr_sem.at[k, d - 1, 0], me, peer),
            remote(lse.at[zd], buf_l.at[k, d - 1], ps_sem.at[k, d, 1], pr_sem.at[k, d - 1, 1], me, peer),
        )

    far = lax.rem(s + 4, NZ)

    @pl.when(s <= 3)
    def _():
        attend(far, False)
        for k, peer in ((0, above), (1, below)):
            for m in p_msgs(far, 4, k, peer, k):
                m.start()

    def ring(i, carry):
        d = 3 - i // 2
        k = lax.rem(i, 2)
        up = k == 0
        zd = jnp.where(up, lax.rem(s + d, NZ), lax.rem(s - d + NZ, NZ))
        peer = jnp.where(up, above, below)
        active = jnp.where(up, s + d, jnp.where(zd >= 4, 0, NZ)) <= NZ - 1
        fresh = active & (zd > s)
        comes = active & ((k == 1) | (s >= 1))

        @pl.when(fresh)
        def _():
            attend(zd, False)

        @pl.when(active & (zd < s))
        def _():
            part[zd] = jnp.zeros((8, 2, SEL, D), BF16)
            lse[zd] = jnp.full((2, 8, D), EMPTY, F32)

        @pl.when(comes & (d == 3))
        def _():
            remote(
                part.at[zd, pl.ds(0, 4)], buf_o.at[k, 3, pl.ds(k * 4, 4)],
                ps_sem.at[k, d, 0], pr_sem.at[k, 3, 0], me, peer,
            ).wait_recv()
            remote(
                lse.at[zd], buf_l.at[k, 3], ps_sem.at[k, d, 1], pr_sem.at[k, 3, 1], me, peer
            ).wait_recv()
            merge(zd, k, k, 3)

        @pl.when(comes & (d < 3))
        def _():
            for m in p_msgs(zd, d + 1, k, peer, None):
                m.wait_recv()
            merge(zd, 0, k, d)
            merge(zd, 1, k, d)

        @pl.when(active)
        def _():
            for m in p_msgs(zd, d, k, peer, None):
                m.start()

        return carry

    lax.fori_loop(0, 6, ring, 0)
    attend(s, True)
    for k, cond in ((0, s >= 1), (1, s >= 4)):

        @pl.when(cond)
        def _(k=k):
            for m in p_msgs(s, 1, k, below, None):
                m.wait_recv()
            merge(s, 0, k, 0)
            merge(s, 1, k, 0)

    fx = remote(part.at[s, :, 1 - c], fin.at[pl.ds(c * 8, 8)], fx_sem.at[0], fx_sem.at[1], me, mate)
    fx.start()
    for h in range(8):
        fin[c * 8 + h] = part[s, h, c]
    remote(
        part.at[s, :, c], fin.at[pl.ds((1 - c) * 8, 8)], fx_sem.at[0], fx_sem.at[1], me, mate
    ).wait_recv()
    for h in range(16):
        att[:, h * D : (h + 1) * D] = fin[h]

    fx.wait_send()
    kx.wait_send()
    qx.wait_send()
    out_copy.wait()
    for i in range(1, NREQ):
        a2a(i).wait_send()
    for t in range(1, 5):
        z_down = s + t - 1
        z_up = lax.rem(s - t + 1 + NZ, NZ)

        @pl.when((z_down <= NZ - 1) & (s >= 1))
        def _(z=z_down, t=t):
            q_msg(z, t, False).wait_send()

        @pl.when(z_up >= 4)
        def _(z=z_up, t=t):
            q_msg(z, t, True).wait_send()

    @pl.when(s <= 3)
    def _():
        for k, peer in ((0, above), (1, below)):
            for m in p_msgs(far, 4, k, peer, k):
                m.wait_send()

    def drain(i, carry):
        d = 3 - i // 2
        k = lax.rem(i, 2)
        up = k == 0
        zd = jnp.where(up, lax.rem(s + d, NZ), lax.rem(s - d + NZ, NZ))
        active = jnp.where(up, s + d, jnp.where(zd >= 4, 0, NZ)) <= NZ - 1

        @pl.when(active)
        def _():
            for m in p_msgs(zd, d, k, above, None):
                m.wait_send()

        return carry

    lax.fori_loop(0, 6, drain, 0)


def body(store, passage_owner, passage_slot, sel_pos, queries, new_kv):
    seq = lax.axis_index("seq")
    chip = seq // 2
    core = seq % 2
    owner = passage_owner[:, :, 0]
    near = lax.dynamic_slice(sel_pos[0], (chip * 2 * SEL,), (2 * SEL,)).reshape(2, SEL) - chip * CHIP_TOK
    own = lax.dynamic_index_in_dim(near, core, 0, keepdims=True) - core * TOK
    pos = jnp.concatenate([own, near], axis=0)
    pos = jnp.pad(pos, ((0, 5), (0, D - SEL)), constant_values=-1).astype(F32)
    vmem = pl.BlockSpec(memory_space=pltpu.VMEM)
    smem = pl.BlockSpec(memory_space=pltpu.SMEM)
    dma = pltpu.SemaphoreType.DMA
    blended, deviation, attended = pl.pallas_call(
        kernel,
        out_shape=(
            jax.ShapeDtypeStruct((TOK, KVW), BF16),
            jax.ShapeDtypeStruct((SEL, 4), F32),
            jax.ShapeDtypeStruct((SEL, QW), BF16),
        ),
        in_specs=[smem, smem, vmem, vmem, vmem, vmem],
        out_specs=(pl.BlockSpec(memory_space=pl.ANY), vmem, vmem),
        scratch_shapes=[
            pltpu.VMEM((NREQ, 2, PASSAGE, KVW), BF16),
            pltpu.VMEM((NREQ, 2, PASSAGE, KVW), BF16),
            pltpu.VMEM((16, SEL, D), BF16),
            pltpu.VMEM((NZ, 8, 2, SEL, D), BF16),
            pltpu.VMEM((TOK, KVW), BF16),
            pltpu.VMEM((TOK, KVW), BF16),
            pltpu.VMEM((2, 2, 2, TOK, D), BF16),
            pltpu.VMEM((2, 2, 2, TOK, D), BF16),
            pltpu.VMEM((NZ, 8, 2, SEL, D), BF16),
            pltpu.VMEM((NZ, 2, 8, D), F32),
            pltpu.VMEM((2, 4, 8, 2, SEL, D), BF16),
            pltpu.VMEM((2, 4, 2, 8, D), F32),
            pltpu.VMEM((16, SEL, D), BF16),
            dma((NREQ,)),
            dma((NREQ,)),
            dma((2,)),
            dma((2, 5)),
            dma((2, 5)),
            dma((2,)),
            dma((2, 5, 2)),
            dma((2, 5, 2)),
            dma((2,)),
            dma,
        ],
        compiler_params=pltpu.CompilerParams(
            collective_id=0, has_side_effects=True, vmem_limit_bytes=60 * 1024 * 1024
        ),
    )(owner, passage_slot, pos, store[:, 0], queries[0], new_kv[0])
    return blended[None], deviation[None], attended[None]


def solution(mesh):
    placed = (
        P("req", "seq", None, None),
        P(None, "seq", None),
        P(None, "seq"),
        P("req", None),
        P("req", "seq", None),
        P("req", "seq", None),
    )
    return jax.shard_map(
        body,
        mesh=mesh,
        in_specs=placed,
        out_specs=(P("req", "seq", None), P("req", "seq", None), P("req", "seq", None)),
        check_vma=False,
    )
```

```python
import math

import jax
import jax.numpy as jnp
from jax import lax
from jax.experimental import pallas as pl
from jax.experimental.pallas import tpu as pltpu
from jax.sharding import PartitionSpec as P

NREQ = 16
NZ = 8
PIECES = 16
PASSAGE = 56
TOK = 896
SEL = 112
KVW = 1024
QW = 2048
D = 128
CHIP_TOK = 2 * TOK
C2 = (D ** -0.5) * math.log2(math.e)
EMPTY = -1e30
F32 = jnp.float32
BF16 = jnp.bfloat16
MESH = pl.DeviceIdType.MESH


def remote(src, dst, ssem, rsem, req, seq):
    return pltpu.make_async_remote_copy(
        src_ref=src,
        dst_ref=dst,
        send_sem=ssem,
        recv_sem=rsem,
        device_id=(req, seq),
        device_id_type=MESH,
    )


RELAYS = (
    ((2, 0), (3, 0), (3, 0)),
    ((0, 2), (0, 3), (0, 3)),
    ((2, 2), (3, 3), (3, 3)),
    ((2, 1), (3, 0), (3, 1)),
    ((1, 2), (1, 3), (0, 3)),
    ((2, 3), (3, 0), (3, 3)),
    ((3, 2), (3, 3), (0, 3)),
)
ROUTES = (
    (2, 2), (2, 0), (0, 2), (2, 1), (1, 2), (2, 3), (3, 2), (1, 1),
    (3, 3), (1, 3), (3, 1), (1, 0), (3, 0), (0, 1), (0, 3),
)
CHUNK = 256


def kernel(
    owner, slot, pos, store, q, fresh_kv,
    blended_out, dev, att,
    outgoing, incoming_0, incoming_1, relayed, qh, qg, cached, blend, bh, kv, part, lse, share,
    buf_o, buf_l, fin, squares,
    a_send, a_recv, l_send, l_recv, f_send, f_recv,
    qx_sem, qs_sem, qr_sem, kx_send, kx_recv, ps_sem, pr_sem, fx_sem, b_sem,
):
    incoming = (incoming_0, incoming_1)
    me = lax.axis_index("req")
    seq = lax.axis_index("seq")
    s = seq // 2
    c = seq % 2
    x = me // 4
    y = me % 4
    mate = s * 2 + (1 - c)
    above = lax.rem(s + 1, NZ) * 2 + c
    below = lax.rem(s + NZ - 1, NZ) * 2 + c

    def to(step):
        return lax.rem(x + step[0], 4) * 4 + lax.rem(y + step[1], 4)

    def back(step):
        return lax.rem(x + 4 - step[0], 4) * 4 + lax.rem(y + 4 - step[1], 4)

    barrier = pltpu.get_barrier_semaphore()
    for step in ROUTES:
        pl.semaphore_signal(barrier, inc=1, device_id=(to(step), seq), device_id_type=MESH)
    for z in (mate, above, below):
        pl.semaphore_signal(barrier, inc=1, device_id=(me, z), device_id_type=MESH)

    for h in range(16):
        qh[h] = q[:, h * D : (h + 1) * D]

    def build(r, carry):
        count = jnp.int32(0)
        first = jnp.int32(0)
        second = jnp.int32(0)
        for j in range(PIECES):
            hit = owner[r, j] == me
            value = slot[r, j]
            first = jnp.where(hit & (count == 0), value, first)
            second = jnp.where(hit & (count == 1), value, second)
            count = count + hit.astype(jnp.int32)
        for k, at in ((0, first), (1, second)):
            piece = store[at]
            for p in range(2):
                for i in range(4):
                    col = (i % 2) * 512 + ((i // 2) * 2 + p) * D
                    outgoing[p, r, k, :, i * D : (i + 1) * D] = piece[:, col : col + D]
        return carry

    lax.fori_loop(0, NREQ, build, 0)
    pl.semaphore_wait(barrier, NREQ - 1 + 3)

    def direct(p, i, arriving):
        step = ROUTES[i]
        other = back(step) if arriving else to(step)
        row = other if arriving else me
        if 2 in step:
            o, n = outgoing.at[p, other, 0], incoming[p].at[row, 0]
        else:
            o, n = outgoing.at[p, other], incoming[p].at[row]
        return remote(o, n, a_send.at[p, i], a_recv.at[p, i], other, seq)

    def leg_one(p, i, arriving):
        target, leg, _ = RELAYS[i]
        other = back(leg) if arriving else to(leg)
        return remote(
            outgoing.at[p, to(target), 1], relayed.at[p, i], l_send.at[p, i], l_recv.at[p, i], other, seq
        )

    def leg_two(p, i, arriving):
        target, leg, last = RELAYS[i]
        other = back(last) if arriving else to(last)
        row = back(target) if arriving else back(leg)
        return remote(
            relayed.at[p, i], incoming[p].at[row, 1], f_send.at[p, i], f_recv.at[p, i], other, seq
        )

    def exchange_start(p):
        for i in range(len(RELAYS)):
            leg_one(p, i, False).start()
        for i in range(len(ROUTES)):
            direct(p, i, False).start()

    def exchange_pass(p):
        for i in range(len(RELAYS)):
            leg_one(p, i, True).wait_recv()
            leg_two(p, i, False).start()

    def q_msg(p, z, t, up):
        k = 1 if up else 0
        if t == 4:
            ref = qg.at[z, pl.ds(p * 4 + 2 * k, 2)]
        else:
            ref = qg.at[z, pl.ds(p * 4, 4)]
        return remote(ref, ref, qs_sem.at[p, k, t], qr_sem.at[p, k, t], me, above if up else below)

    def q_arrive(p, t):
        z_down = s + t
        z_up = lax.rem(s - t + NZ, NZ)

        @pl.when(z_down <= NZ - 1)
        def _():
            q_msg(p, z_down, t, False).wait_recv()

        @pl.when(z_up >= 4)
        def _():
            q_msg(p, z_up, t, True).wait_recv()

    def q_leave(p, t, over):
        z_down = s + t - 1
        z_up = lax.rem(s - t + 1 + NZ, NZ)

        @pl.when((z_down <= NZ - 1) & (s >= 1))
        def _():
            m = q_msg(p, z_down, t, False)
            m.wait_send() if over else m.start()

        @pl.when(z_up >= 4)
        def _():
            m = q_msg(p, z_up, t, True)
            m.wait_send() if over else m.start()

    qx = remote(qh.at[pl.ds((1 - c) * 8, 8)], qg.at[s, :, c], qx_sem.at[0], qx_sem.at[1], me, mate)
    qx.start()
    exchange_start(0)
    for h in range(8):
        qg[s, h, c] = qh[c * 8 + h]
    remote(qh.at[pl.ds(0, 8)], qg.at[s, :, 1 - c], qx_sem.at[0], qx_sem.at[1], me, mate).wait_recv()
    q_leave(0, 1, False)
    for p in range(2):
        incoming[p][me] = outgoing[p, me]

    eye = lax.broadcasted_iota(jnp.int32, (SEL, D), 0) == lax.broadcasted_iota(jnp.int32, (SEL, D), 1)

    def to_col(row):
        return jnp.sum(jnp.where(eye, row, 0.0), axis=1, keepdims=True)

    def to_row(col):
        return jnp.sum(jnp.where(eye, col, 0.0), axis=0, keepdims=True)

    exchange_pass(0)
    exchange_start(1)
    for t in range(2, 5):
        q_arrive(0, t - 1)
        q_leave(0, t, False)
    q_leave(1, 1, False)
    q_arrive(0, 4)

    def gathered(p):
        for i in range(len(ROUTES)):
            direct(p, i, True).wait_recv()
        for i in range(len(RELAYS)):
            leg_two(p, i, True).wait_recv()
        mine = [owner[me, j] for j in range(PIECES)]
        for j in range(PIECES):
            rank = jnp.int32(0)
            for k in range(j):
                rank = rank + (mine[k] == mine[j]).astype(jnp.int32)
            cached[j * PASSAGE : (j + 1) * PASSAGE, :] = incoming[p][mine[j], jnp.minimum(rank, 1)]

    def blend_in(p):
        own_row = pos[0:1, :]
        index = lax.broadcasted_iota(jnp.int32, (SEL, TOK), 1).astype(F32)
        pick = jnp.where(index == to_col(own_row), 1.0, 0.0).astype(BF16)
        put = jnp.where(lax.broadcasted_iota(jnp.int32, (TOK, D), 0).astype(F32) == own_row, 1.0, 0.0)
        hit_col = jnp.sum(put, axis=1, keepdims=True) > 0.5
        put = put.astype(BF16)[:, :SEL]
        for core in range(2):
            total = None
            for k in range(2):
                cols = pl.ds(pl.multiple_of(k * 512 + (core * 2 + p) * D, D), D)
                old = cached[:, (core * 2 + k) * D : (core * 2 + k + 1) * D]
                new = fresh_kv[:, cols]
                placed = jnp.dot(put, new, preferred_element_type=F32)
                both = jnp.where(hit_col, placed, old.astype(F32)).astype(BF16)
                blend[:, cols] = both
                bh[p, core, k] = both
                diff = new.astype(F32) - jnp.dot(pick, old, preferred_element_type=F32)
                total = diff * diff if total is None else total + diff * diff
            squares[core * 2 + p] = total

    def keys_msg(p, arriving):
        if arriving:
            return remote(bh.at[p, c], kv.at[p, :, 1 - c], kx_send.at[p], kx_recv.at[p], me, mate)
        return remote(bh.at[p, 1 - c], kv.at[p, :, c], kx_send.at[p], kx_recv.at[p], me, mate)

    def attend(zd, p, masked):
        rows = qg[zd, pl.ds(p * 4, 4)].reshape(8 * SEL, D)
        if masked:
            limit = [to_col(pos[1:2, :]), to_col(pos[2:3, :])]
            limit = jnp.concatenate(limit * 4, axis=0)
        top = total = product = None
        for i in range(CHIP_TOK // CHUNK):
            at = i * CHUNK
            keys = [kv[p, 0].reshape(CHIP_TOK, D)[at : at + CHUNK], kv[p, 1].reshape(CHIP_TOK, D)[at : at + CHUNK]]
            scores = lax.dot_general(
                rows, keys[0], (((1,), (1,)), ((), ())), preferred_element_type=F32
            )
            if masked:
                index = lax.broadcasted_iota(jnp.int32, (8 * SEL, CHUNK), 1).astype(F32) + float(at)
                scores = jnp.where(index <= limit, scores, EMPTY)
            high = jnp.max(scores, axis=1, keepdims=True)
            if top is not None:
                high = jnp.maximum(top, high)
            weights = jnp.exp2((scores - high) * C2)
            sums = weights[:, :D] + weights[:, D:]
            now = jnp.dot(weights.astype(BF16), keys[1], preferred_element_type=F32)
            if top is None:
                total, product = sums, now
            else:
                shrink = jnp.exp2((top - high) * C2)
                total = total * shrink + sums
                product = product * shrink + now
            top = high
        total = jnp.sum(total, axis=1, keepdims=True)
        part[zd, pl.ds(p * 4, 4)] = (product / total).astype(BF16).reshape(4, 2, SEL, D)
        level = top * C2 + jnp.log2(total)
        for g in range(8):
            lse[zd, p, g : g + 1, :] = to_row(level[g * SEL : (g + 1) * SEL])

    def merge(zd, p, k, at, half):
        have = lse[zd, p]
        came = buf_l[k, at, p]
        if half:
            row = lax.broadcasted_iota(jnp.int32, (8, D), 0) // 4
            came = jnp.where(row == k, came, EMPTY)
        high = jnp.maximum(have, came)
        e_have = jnp.exp2(have - high)
        e_came = jnp.exp2(came - high)
        total = e_have + e_came
        share[...] = e_came / total
        lse[zd, p] = high + jnp.log2(total)

        def one(g, carry):
            for b in range(2):
                w = to_col(share[pl.ds(g * 2 + b, 1), :])
                a = part[zd, p * 4 + g, b].astype(F32)
                n = buf_o[k, at, p * 4 + g, b].astype(F32)
                part[zd, p * 4 + g, b] = (a + w * (n - a)).astype(BF16)
            return carry

        if half:
            for g in range(2):
                one(k * 2 + g, 0)
        else:
            for g in range(4):
                one(g, 0)

    def p_msgs(zd, p, d, k, peer, half):
        heads = pl.ds(p * 4 + k * 2, 2) if half else pl.ds(p * 4, 4)
        return (
            remote(
                part.at[zd, heads], buf_o.at[k, d - 1, heads],
                ps_sem.at[p, k, d, 0], pr_sem.at[p, k, d - 1, 0], me, peer,
            ),
            remote(
                lse.at[zd, p], buf_l.at[k, d - 1, p],
                ps_sem.at[p, k, d, 1], pr_sem.at[p, k, d - 1, 1], me, peer,
            ),
        )

    far = lax.rem(s + 4, NZ)

    def phase(p, whole):
        for n in range(2):

            @pl.when(p == n)
            def _(n=n):
                gathered(n)

        blend_in(p)
        keys_msg(p, False).start()
        for k in range(2):
            kv[p, k, c] = bh[p, c, k]

        @pl.when(p == 0)
        def _():
            exchange_pass(1)

        @pl.when(p == 1)
        def _():
            q_arrive(1, 4)

        keys_msg(p, True).wait_recv()

        @pl.when(s <= 3)
        def _():
            attend(far, p, False)
            for k, peer in ((0, above), (1, below)):
                for m in p_msgs(far, p, 4, k, peer, True):
                    m.start()

        def ring(i, carry):
            d = 3 - i // 2
            k = lax.rem(i, 2)
            up = k == 0
            zd = jnp.where(up, lax.rem(s + d, NZ), lax.rem(s - d + NZ, NZ))
            peer = jnp.where(up, above, below)
            active = jnp.where(up, s + d, jnp.where(zd >= 4, 0, NZ)) <= NZ - 1
            comes = active & ((k == 1) | (s >= 1))

            for n in range(3):

                @pl.when((p == 0) & (i == 2 * n))
                def _(n=n):
                    q_arrive(1, n + 1)
                    q_leave(1, n + 2, False)

            @pl.when(active & (zd > s))
            def _():
                attend(zd, p, False)

            @pl.when(active & (zd < s))
            def _():
                part[zd, pl.ds(p * 4, 4)] = jnp.zeros((4, 2, SEL, D), BF16)
                lse[zd, p] = jnp.full((8, D), EMPTY, F32)

            @pl.when(comes & (d == 3))
            def _():
                for m in p_msgs(zd, p, 4, k, peer, True):
                    m.wait_recv()
                merge(zd, p, k, 3, True)

            @pl.when(comes & (d < 3))
            def _():
                for m in p_msgs(zd, p, d + 1, k, peer, False):
                    m.wait_recv()
                merge(zd, p, k, d, False)

            @pl.when(active)
            def _():
                for m in p_msgs(zd, p, d, k, peer, False):
                    m.start()

            return carry

        lax.fori_loop(0, 6, ring, 0)
        attend(s, p, True)
        return whole

    lax.fori_loop(0, 2, phase, 0)
    out_copy = pltpu.make_async_copy(blend, blended_out, b_sem)
    out_copy.start()
    for h in range(4):
        dev[:, h : h + 1] = jnp.sum(squares[h], axis=1, keepdims=True)

    def finish(p, carry):
        for k, cond in ((0, s >= 1), (1, s >= 4)):

            @pl.when(cond)
            def _(k=k):
                for m in p_msgs(s, p, 1, k, below, False):
                    m.wait_recv()
                merge(s, p, k, 0, False)

        return carry

    lax.fori_loop(0, 2, finish, 0)
    fx = remote(part.at[s, :, 1 - c], fin.at[pl.ds(c * 8, 8)], fx_sem.at[0], fx_sem.at[1], me, mate)
    fx.start()
    for h in range(8):
        fin[c * 8 + h] = part[s, h, c]

    def drain(p, carry):
        keys_msg(p, False).wait_send()
        for t in range(1, 5):
            q_leave(p, t, True)

        @pl.when(s <= 3)
        def _():
            for k, peer in ((0, above), (1, below)):
                for m in p_msgs(far, p, 4, k, peer, True):
                    m.wait_send()

        def sent(i, inner):
            d = 3 - i // 2
            k = lax.rem(i, 2)
            up = k == 0
            zd = jnp.where(up, lax.rem(s + d, NZ), lax.rem(s - d + NZ, NZ))
            active = jnp.where(up, s + d, jnp.where(zd >= 4, 0, NZ)) <= NZ - 1

            @pl.when(active)
            def _():
                for m in p_msgs(zd, p, d, k, above, False):
                    m.wait_send()

            return inner

        lax.fori_loop(0, 6, sent, 0)
        return carry

    lax.fori_loop(0, 2, drain, 0)
    for p in range(2):
        for i in range(len(ROUTES)):
            direct(p, i, False).wait_send()
        for i in range(len(RELAYS)):
            leg_one(p, i, False).wait_send()
            leg_two(p, i, False).wait_send()
    qx.wait_send()
    remote(
        part.at[s, :, c], fin.at[pl.ds((1 - c) * 8, 8)], fx_sem.at[0], fx_sem.at[1], me, mate
    ).wait_recv()
    for h in range(16):
        att[:, h * D : (h + 1) * D] = fin[h]
    fx.wait_send()
    out_copy.wait()


def body(store, passage_owner, passage_slot, sel_pos, queries, new_kv):
    seq = lax.axis_index("seq")
    chip = seq // 2
    core = seq % 2
    owner = passage_owner[:, :, 0]
    near = lax.dynamic_slice(sel_pos[0], (chip * 2 * SEL,), (2 * SEL,)).reshape(2, SEL) - chip * CHIP_TOK
    own = lax.dynamic_index_in_dim(near, core, 0, keepdims=True) - core * TOK
    pos = jnp.concatenate([own, near], axis=0)
    pos = jnp.pad(pos, ((0, 5), (0, D - SEL)), constant_values=-1).astype(F32)
    vmem = pl.BlockSpec(memory_space=pltpu.VMEM)
    smem = pl.BlockSpec(memory_space=pltpu.SMEM)
    dma = pltpu.SemaphoreType.DMA
    blended, deviation, attended = pl.pallas_call(
        kernel,
        out_shape=(
            jax.ShapeDtypeStruct((TOK, KVW), BF16),
            jax.ShapeDtypeStruct((SEL, 4), F32),
            jax.ShapeDtypeStruct((SEL, QW), BF16),
        ),
        in_specs=[smem, smem, vmem, vmem, vmem, vmem],
        out_specs=(pl.BlockSpec(memory_space=pl.ANY), vmem, vmem),
        scratch_shapes=[
            pltpu.VMEM((2, NREQ, 2, PASSAGE, KVW // 2), BF16),
            pltpu.VMEM((NREQ, 2, PASSAGE, KVW // 2), BF16),
            pltpu.VMEM((NREQ, 2, PASSAGE, KVW // 2), BF16),
            pltpu.VMEM((2, len(RELAYS), PASSAGE, KVW // 2), BF16),
            pltpu.VMEM((16, SEL, D), BF16),
            pltpu.VMEM((NZ, 8, 2, SEL, D), BF16),
            pltpu.VMEM((TOK, KVW // 2), BF16),
            pltpu.VMEM((TOK, KVW), BF16),
            pltpu.VMEM((2, 2, 2, TOK, D), BF16),
            pltpu.VMEM((2, 2, 2, TOK, D), BF16),
            pltpu.VMEM((NZ, 8, 2, SEL, D), BF16),
            pltpu.VMEM((NZ, 2, 8, D), F32),
            pltpu.VMEM((8, D), F32),
            pltpu.VMEM((2, 4, 8, 2, SEL, D), BF16),
            pltpu.VMEM((2, 4, 2, 8, D), F32),
            pltpu.VMEM((16, SEL, D), BF16),
            pltpu.VMEM((4, SEL, D), F32),
            dma((2, len(ROUTES))),
            dma((2, len(ROUTES))),
            dma((2, len(RELAYS))),
            dma((2, len(RELAYS))),
            dma((2, len(RELAYS))),
            dma((2, len(RELAYS))),
            dma((2,)),
            dma((2, 2, 5)),
            dma((2, 2, 5)),
            dma((2,)),
            dma((2,)),
            dma((2, 2, 5, 2)),
            dma((2, 2, 5, 2)),
            dma((2,)),
            dma,
        ],
        compiler_params=pltpu.CompilerParams(
            collective_id=0, has_side_effects=True, vmem_limit_bytes=60 * 1024 * 1024
        ),
    )(owner, passage_slot, pos, store[:, 0], queries[0], new_kv[0])
    return blended[None], deviation[None], attended[None]


def solution(mesh):
    placed = (
        P("req", "seq", None, None),
        P(None, "seq", None),
        P(None, "seq"),
        P("req", None),
        P("req", "seq", None),
        P("req", "seq", None),
    )
    return jax.shard_map(
        body,
        mesh=mesh,
        in_specs=placed,
        out_specs=(P("req", "seq", None), P("req", "seq", None), P("req", "seq", None)),
        check_vma=False,
    )
```

```python
import math

import jax
import jax.numpy as jnp
from jax import lax
from jax.experimental import pallas as pl
from jax.experimental.pallas import tpu as pltpu
from jax.sharding import PartitionSpec as P

NREQ = 16
NZ = 8
PIECES = 16
PASSAGE = 56
TOK = 896
SEL = 112
KVW = 1024
QW = 2048
D = 128
CHIP_TOK = 2 * TOK
C2 = (D ** -0.5) * math.log2(math.e)
EMPTY = -1e30
F32 = jnp.float32
BF16 = jnp.bfloat16
MESH = pl.DeviceIdType.MESH


def remote(src, dst, ssem, rsem, req, seq):
    return pltpu.make_async_remote_copy(
        src_ref=src,
        dst_ref=dst,
        send_sem=ssem,
        recv_sem=rsem,
        device_id=(req, seq),
        device_id_type=MESH,
    )


ROUTES = (
    (1, 0), (3, 0), (0, 1), (0, 3), (2, 0), (0, 2), (1, 1), (3, 3),
    (1, 3), (3, 1), (2, 1), (1, 2), (2, 3), (3, 2), (2, 2),
)
CHUNK = 256


def kernel(
    owner, slot, pos, store, q, fresh_kv,
    blended_out, dev, att,
    outgoing, incoming_0, incoming_1, qh, qg, cached, blend, bh, kv, part, lse,
    buf_o, buf_l, fin, squares,
    a_send, a_recv,
    qx_sem, qs_sem, qr_sem, kx_send, kx_recv, ps_sem, pr_sem, fx_sem, b_sem,
):
    incoming = (incoming_0, incoming_1)
    me = lax.axis_index("req")
    seq = lax.axis_index("seq")
    s = seq // 2
    c = seq % 2
    x = me // 4
    y = me % 4
    mate = s * 2 + (1 - c)
    above = lax.rem(s + 1, NZ) * 2 + c
    below = lax.rem(s + NZ - 1, NZ) * 2 + c

    def to(step):
        dx = jnp.where(c == 0, step[0], 4 - step[0])
        dy = jnp.where(c == 0, step[1], 4 - step[1])
        return lax.rem(x + dx, 4) * 4 + lax.rem(y + dy, 4)

    def back(step):
        return to((4 - step[0], 4 - step[1]))

    barrier = pltpu.get_barrier_semaphore()
    for step in ROUTES:
        pl.semaphore_signal(barrier, inc=1, device_id=(to(step), seq), device_id_type=MESH)
    for z in (mate, above, below):
        pl.semaphore_signal(barrier, inc=1, device_id=(me, z), device_id_type=MESH)

    for h in range(16):
        qh[h] = q[:, h * D : (h + 1) * D]

    def build(r, carry):
        count = jnp.int32(0)
        first = jnp.int32(0)
        second = jnp.int32(0)
        for j in range(PIECES):
            hit = owner[r, j] == me
            value = slot[r, j]
            first = jnp.where(hit & (count == 0), value, first)
            second = jnp.where(hit & (count == 1), value, second)
            count = count + hit.astype(jnp.int32)
        for k, at in ((0, first), (1, second)):
            piece = store[at]
            for p in range(2):
                for i in range(4):
                    col = (i % 2) * 512 + ((i // 2) * 2 + p) * D
                    outgoing[p, r, k, :, i * D : (i + 1) * D] = piece[:, col : col + D]
        return carry

    lax.fori_loop(0, NREQ, build, 0)
    pl.semaphore_wait(barrier, NREQ - 1 + 3)

    def direct(p, i, arriving):
        other = back(ROUTES[i]) if arriving else to(ROUTES[i])
        row = other if arriving else me
        return remote(
            outgoing.at[p, other], incoming[p].at[row], a_send.at[p, i], a_recv.at[p, i], other, seq
        )

    def exchange_start(p):
        for i in range(len(ROUTES)):
            direct(p, i, False).start()

    def q_msg(p, h, z, t, up):
        k = 1 if up else 0
        ref = qg.at[z, pl.ds(p * 4 + 2 * h, 2)]
        return remote(
            ref, ref, qs_sem.at[p, h, k, t], qr_sem.at[p, h, k, t], me, above if up else below
        )

    def q_arrive(p, h, t):
        z_down = s + t
        z_up = lax.rem(s - t + NZ, NZ)
        if t < 4 or h == 0:

            @pl.when(z_down <= NZ - 1)
            def _():
                q_msg(p, h, z_down, t, False).wait_recv()

        if t < 4 or h == 1:

            @pl.when(z_up >= 4)
            def _():
                q_msg(p, h, z_up, t, True).wait_recv()

    def q_leave(p, h, t, over):
        z_down = s + t - 1
        z_up = lax.rem(s - t + 1 + NZ, NZ)
        if t < 4 or h == 0:

            @pl.when((z_down <= NZ - 1) & (s >= 1))
            def _():
                m = q_msg(p, h, z_down, t, False)
                m.wait_send() if over else m.start()

        if t < 4 or h == 1:

            @pl.when(z_up >= 4)
            def _():
                m = q_msg(p, h, z_up, t, True)
                m.wait_send() if over else m.start()

    qx = remote(qh.at[pl.ds((1 - c) * 8, 8)], qg.at[s, :, c], qx_sem.at[0], qx_sem.at[1], me, mate)
    qx.start()
    exchange_start(0)
    exchange_start(1)
    for h in range(8):
        qg[s, h, c] = qh[c * 8 + h]
    remote(qh.at[pl.ds(0, 8)], qg.at[s, :, 1 - c], qx_sem.at[0], qx_sem.at[1], me, mate).wait_recv()
    for h in range(2):
        q_leave(0, h, 1, False)
    for p in range(2):
        incoming[p][me] = outgoing[p, me]

    eye = lax.broadcasted_iota(jnp.int32, (SEL, D), 0) == lax.broadcasted_iota(jnp.int32, (SEL, D), 1)

    def to_col(row):
        return jnp.sum(jnp.where(eye, row, 0.0), axis=1, keepdims=True)

    def to_row(col):
        return jnp.sum(jnp.where(eye, col, 0.0), axis=0, keepdims=True)

    for t in range(2, 5):
        for h in range(2):
            q_arrive(0, h, t - 1)
            q_leave(0, h, t, False)
    for h in range(2):
        q_leave(1, h, 1, False)
    for h in range(2):
        q_arrive(0, h, 4)

    def gathered(p):
        for i in range(len(ROUTES)):
            direct(p, i, True).wait_recv()
        mine = [owner[me, j] for j in range(PIECES)]
        for j in range(PIECES):
            rank = jnp.int32(0)
            for k in range(j):
                rank = rank + (mine[k] == mine[j]).astype(jnp.int32)
            cached[j * PASSAGE : (j + 1) * PASSAGE, :] = incoming[p][mine[j], jnp.minimum(rank, 1)]

    def blend_in(p):
        own_row = pos[0:1, :]
        index = lax.broadcasted_iota(jnp.int32, (SEL, TOK), 1).astype(F32)
        pick = jnp.where(index == to_col(own_row), 1.0, 0.0).astype(BF16)
        put = jnp.where(lax.broadcasted_iota(jnp.int32, (TOK, D), 0).astype(F32) == own_row, 1.0, 0.0)
        hit_col = jnp.sum(put, axis=1, keepdims=True) > 0.5
        put = put.astype(BF16)[:, :SEL]
        for core in range(2):
            total = None
            for k in range(2):
                cols = pl.ds(pl.multiple_of(k * 512 + (core * 2 + p) * D, D), D)
                old = cached[:, (core * 2 + k) * D : (core * 2 + k + 1) * D]
                new = fresh_kv[:, cols]
                placed = jnp.dot(put, new, preferred_element_type=F32)
                both = jnp.where(hit_col, placed, old.astype(F32)).astype(BF16)
                blend[:, cols] = both
                bh[p, core, k] = both
                diff = new.astype(F32) - jnp.dot(pick, old, preferred_element_type=F32)
                total = diff * diff if total is None else total + diff * diff
            squares[core * 2 + p] = total

    def keys_msg(p, arriving):
        if arriving:
            return remote(bh.at[p, c], kv.at[p, :, 1 - c], kx_send.at[p], kx_recv.at[p], me, mate)
        return remote(bh.at[p, 1 - c], kv.at[p, :, c], kx_send.at[p], kx_recv.at[p], me, mate)

    def attend(zd, p, masked):
        rows = qg[zd, pl.ds(p * 4, 4)].reshape(8 * SEL, D)
        if masked:
            limit = [to_col(pos[1:2, :]), to_col(pos[2:3, :])]
            limit = jnp.concatenate(limit * 4, axis=0)
        top = total = product = None
        for i in range(CHIP_TOK // CHUNK):
            at = i * CHUNK
            keys = [kv[p, 0].reshape(CHIP_TOK, D)[at : at + CHUNK], kv[p, 1].reshape(CHIP_TOK, D)[at : at + CHUNK]]
            scores = lax.dot_general(
                rows, keys[0], (((1,), (1,)), ((), ())), preferred_element_type=F32
            )
            if masked:
                index = lax.broadcasted_iota(jnp.int32, (8 * SEL, CHUNK), 1).astype(F32) + float(at)
                scores = jnp.where(index <= limit, scores, EMPTY)
            high = jnp.max(scores, axis=1, keepdims=True)
            if top is not None:
                high = jnp.maximum(top, high)
            weights = jnp.exp2((scores - high) * C2)
            sums = weights[:, :D] + weights[:, D:]
            now = jnp.dot(weights.astype(BF16), keys[1], preferred_element_type=F32)
            if top is None:
                total, product = sums, now
            else:
                shrink = jnp.exp2((top - high) * C2)
                total = total * shrink + sums
                product = product * shrink + now
            top = high
        total = jnp.sum(total, axis=1, keepdims=True)
        part[zd, pl.ds(p * 4, 4)] = (product / total).astype(BF16).reshape(4, 2, SEL, D)
        level = top * C2 + jnp.log2(total)
        for g in range(8):
            lse[zd, p, g // 4, g % 4 : g % 4 + 1, :] = to_row(level[g * SEL : (g + 1) * SEL])

    def merge(zd, p, k, at, h):
        have = lse[zd, p, h]
        came = buf_l[k, at, p, h]
        high = jnp.maximum(have, came)
        e_have = jnp.exp2(have - high)
        e_came = jnp.exp2(came - high)
        total = e_have + e_came
        part_of = e_came / total
        lse[zd, p, h] = high + jnp.log2(total)
        for g in range(2):
            for b in range(2):
                w = to_col(part_of[g * 2 + b : g * 2 + b + 1, :])
                a = part[zd, p * 4 + h * 2 + g, b].astype(F32)
                n = buf_o[k, at, p * 4 + h * 2 + g, b].astype(F32)
                part[zd, p * 4 + h * 2 + g, b] = (a + w * (n - a)).astype(BF16)

    def p_msgs(zd, p, d, k, h, peer):
        heads = pl.ds(p * 4 + h * 2, 2)
        return (
            remote(
                part.at[zd, heads], buf_o.at[k, d - 1, heads],
                ps_sem.at[p, k, d, h, 0], pr_sem.at[p, k, d - 1, h, 0], me, peer,
            ),
            remote(
                lse.at[zd, p, h], buf_l.at[k, d - 1, p, h],
                ps_sem.at[p, k, d, h, 1], pr_sem.at[p, k, d - 1, h, 1], me, peer,
            ),
        )

    far = lax.rem(s + 4, NZ)

    def phase(p, whole):
        for n in range(2):

            @pl.when(p == n)
            def _(n=n):
                gathered(n)

        blend_in(p)
        keys_msg(p, False).start()
        for k in range(2):
            kv[p, k, c] = bh[p, c, k]

        @pl.when(p == 1)
        def _():
            for h in range(2):
                q_arrive(1, h, 4)

        keys_msg(p, True).wait_recv()

        @pl.when(s <= 3)
        def _():
            attend(far, p, False)
            for k, peer in ((0, above), (1, below)):
                for m in p_msgs(far, p, 4, k, k, peer):
                    m.start()

        def ring(i, carry):
            d = 3 - i // 2
            k = lax.rem(i, 2)
            up = k == 0
            zd = jnp.where(up, lax.rem(s + d, NZ), lax.rem(s - d + NZ, NZ))
            peer = jnp.where(up, above, below)
            active = jnp.where(up, s + d, jnp.where(zd >= 4, 0, NZ)) <= NZ - 1
            comes = active & ((k == 1) | (s >= 1))

            for n in range(3):

                @pl.when((p == 0) & (i == 2 * n))
                def _(n=n):
                    for h in range(2):
                        q_arrive(1, h, n + 1)
                        q_leave(1, h, n + 2, False)

            @pl.when(active & (zd > s))
            def _():
                attend(zd, p, False)

            @pl.when(active & (zd < s))
            def _():
                part[zd, pl.ds(p * 4, 4)] = jnp.zeros((4, 2, SEL, D), BF16)
                lse[zd, p] = jnp.full((2, 4, D), EMPTY, F32)

            def pass_on(h, inner):
                @pl.when(comes & ((d < 3) | (h == k)))
                def _():
                    for m in p_msgs(zd, p, d + 1, k, h, peer):
                        m.wait_recv()
                    merge(zd, p, k, d, h)

                @pl.when(active)
                def _():
                    for m in p_msgs(zd, p, d, k, h, peer):
                        m.start()

                return inner

            lax.fori_loop(0, 2, pass_on, 0)
            return carry

        lax.fori_loop(0, 6, ring, 0)
        attend(s, p, True)
        return whole

    lax.fori_loop(0, 2, phase, 0)
    out_copy = pltpu.make_async_copy(blend, blended_out, b_sem)
    out_copy.start()
    for h in range(4):
        dev[h : h + 1, :] = to_row(jnp.sum(squares[h], axis=1, keepdims=True))[:, :SEL]

    def finish(p, carry):
        for k, cond in ((0, s >= 1), (1, s >= 4)):

            @pl.when(cond)
            def _(k=k):
                for h in range(2):
                    for m in p_msgs(s, p, 1, k, h, below):
                        m.wait_recv()
                    merge(s, p, k, 0, h)

        return carry

    lax.fori_loop(0, 2, finish, 0)
    fx = remote(part.at[s, :, 1 - c], fin.at[pl.ds(c * 8, 8)], fx_sem.at[0], fx_sem.at[1], me, mate)
    fx.start()
    for h in range(8):
        fin[c * 8 + h] = part[s, h, c]

    def drain(p, carry):
        keys_msg(p, False).wait_send()
        for t in range(1, 5):
            for h in range(2):
                q_leave(p, h, t, True)

        @pl.when(s <= 3)
        def _():
            for k, peer in ((0, above), (1, below)):
                for m in p_msgs(far, p, 4, k, k, peer):
                    m.wait_send()

        def sent(i, inner):
            d = 3 - i // 2
            k = lax.rem(i, 2)
            up = k == 0
            zd = jnp.where(up, lax.rem(s + d, NZ), lax.rem(s - d + NZ, NZ))
            active = jnp.where(up, s + d, jnp.where(zd >= 4, 0, NZ)) <= NZ - 1

            @pl.when(active)
            def _():
                for h in range(2):
                    for m in p_msgs(zd, p, d, k, h, above):
                        m.wait_send()

            return inner

        lax.fori_loop(0, 6, sent, 0)
        return carry

    lax.fori_loop(0, 2, drain, 0)
    for p in range(2):
        for i in range(len(ROUTES)):
            direct(p, i, False).wait_send()
    qx.wait_send()
    remote(
        part.at[s, :, c], fin.at[pl.ds((1 - c) * 8, 8)], fx_sem.at[0], fx_sem.at[1], me, mate
    ).wait_recv()
    for h in range(16):
        att[:, h * D : (h + 1) * D] = fin[h]
    fx.wait_send()
    out_copy.wait()


def hand_on(a_in, b_in, c_in, a_out, b_out, c_out, a_mid, b_mid, c_mid, sem_in, sem_out):
    ways = ((a_in, a_mid, a_out), (b_in, b_mid, b_out), (c_in, c_mid, c_out))
    taken = [pltpu.make_async_copy(w[0], w[1], sem_in.at[i]) for i, w in enumerate(ways)]
    given = [pltpu.make_async_copy(w[1], w[2], sem_out.at[i]) for i, w in enumerate(ways)]
    for copy in taken:
        copy.start()
    for first, then in zip(taken, given):
        first.wait()
        then.start()
    for copy in given:
        copy.wait()


def body(store, passage_owner, passage_slot, sel_pos, queries, new_kv):
    seq = lax.axis_index("seq")
    chip = seq // 2
    core = seq % 2
    owner = passage_owner[:, :, 0]
    near = lax.dynamic_slice(sel_pos[0], (chip * 2 * SEL,), (2 * SEL,)).reshape(2, SEL) - chip * CHIP_TOK
    own = lax.dynamic_index_in_dim(near, core, 0, keepdims=True) - core * TOK
    pos = jnp.concatenate([own, near], axis=0)
    pos = jnp.pad(pos, ((0, 5), (0, D - SEL)), constant_values=-1).astype(F32)
    vmem = pl.BlockSpec(memory_space=pltpu.VMEM)
    smem = pl.BlockSpec(memory_space=pltpu.SMEM)
    dma = pltpu.SemaphoreType.DMA
    blended, deviation, attended = pl.pallas_call(
        kernel,
        out_shape=(
            jax.ShapeDtypeStruct((TOK, KVW), BF16),
            jax.ShapeDtypeStruct((4, SEL), F32),
            jax.ShapeDtypeStruct((SEL, QW), BF16),
        ),
        in_specs=[smem, smem, vmem, vmem, vmem, vmem],
        out_specs=(pl.BlockSpec(memory_space=pl.ANY), vmem, vmem),
        scratch_shapes=[
            pltpu.VMEM((2, NREQ, 2, PASSAGE, KVW // 2), BF16),
            pltpu.VMEM((NREQ, 2, PASSAGE, KVW // 2), BF16),
            pltpu.VMEM((NREQ, 2, PASSAGE, KVW // 2), BF16),
            pltpu.VMEM((16, SEL, D), BF16),
            pltpu.VMEM((NZ, 8, 2, SEL, D), BF16),
            pltpu.VMEM((TOK, KVW // 2), BF16),
            pltpu.VMEM((TOK, KVW), BF16),
            pltpu.VMEM((2, 2, 2, TOK, D), BF16),
            pltpu.VMEM((2, 2, 2, TOK, D), BF16),
            pltpu.VMEM((NZ, 8, 2, SEL, D), BF16),
            pltpu.VMEM((NZ, 2, 2, 4, D), F32),
            pltpu.VMEM((2, 4, 8, 2, SEL, D), BF16),
            pltpu.VMEM((2, 4, 2, 2, 4, D), F32),
            pltpu.VMEM((16, SEL, D), BF16),
            pltpu.VMEM((4, SEL, D), F32),
            dma((2, len(ROUTES))),
            dma((2, len(ROUTES))),
            dma((2,)),
            dma((2, 2, 2, 5)),
            dma((2, 2, 2, 5)),
            dma((2,)),
            dma((2,)),
            dma((2, 2, 5, 2, 2)),
            dma((2, 2, 5, 2, 2)),
            dma((2,)),
            dma,
        ],
        compiler_params=pltpu.CompilerParams(
            collective_id=0, has_side_effects=True, vmem_limit_bytes=60 * 1024 * 1024
        ),
    )(owner, passage_slot, pos, store[:, 0], queries[0], new_kv[0])
    blended, deviation, attended = pl.pallas_call(
        hand_on,
        out_shape=(
            jax.ShapeDtypeStruct((TOK, KVW), BF16),
            jax.ShapeDtypeStruct((4, SEL), F32),
            jax.ShapeDtypeStruct((SEL, QW), BF16),
        ),
        in_specs=[pl.BlockSpec(memory_space=pl.ANY)] * 3,
        out_specs=(pl.BlockSpec(memory_space=pl.ANY),) * 3,
        scratch_shapes=[
            pltpu.VMEM((TOK, KVW), BF16),
            pltpu.VMEM((4, SEL), F32),
            pltpu.VMEM((SEL, QW), BF16),
            dma((3,)),
            dma((3,)),
        ],
    )(blended, deviation, attended)
    return blended[None], deviation.T[None], attended[None]


def solution(mesh):
    placed = (
        P("req", "seq", None, None),
        P(None, "seq", None),
        P(None, "seq"),
        P("req", None),
        P("req", "seq", None),
        P("req", "seq", None),
    )
    return jax.shard_map(
        body,
        mesh=mesh,
        in_specs=placed,
        out_specs=(P("req", "seq", None), P("req", "seq", None), P("req", "seq", None)),
        check_vma=False,
    )
```

```python
import math

import jax
import jax.numpy as jnp
from jax import lax
from jax.experimental import pallas as pl
from jax.experimental.pallas import tpu as pltpu
from jax.sharding import PartitionSpec as P

NREQ = 16
NZ = 8
PIECES = 16
PASSAGE = 56
TOK = 896
SEL = 112
KVW = 1024
QW = 2048
D = 128
CHIP_TOK = 2 * TOK
C2 = (D ** -0.5) * math.log2(math.e)
EMPTY = -1e30
F32 = jnp.float32
BF16 = jnp.bfloat16
MESH = pl.DeviceIdType.MESH


def remote(src, dst, ssem, rsem, req, seq):
    return pltpu.make_async_remote_copy(
        src_ref=src,
        dst_ref=dst,
        send_sem=ssem,
        recv_sem=rsem,
        device_id=(req, seq),
        device_id_type=MESH,
    )


ROUTES = (
    (1, 0), (3, 0), (0, 1), (0, 3), (2, 0), (0, 2), (1, 1), (3, 3),
    (1, 3), (3, 1), (2, 1), (1, 2), (2, 3), (3, 2), (2, 2),
)
CHUNK = 256


def kernel(
    owner, slot, pos, store, q, fresh_kv,
    blended_out, dev, att,
    outgoing, incoming_0, incoming_1, qh, qg, cached, blend, bh, kv, part, lse,
    buf_o, buf_l, fin, squares,
    a_send, a_recv,
    qx_sem, qs_sem, qr_sem, kx_send, kx_recv, ps_sem, pr_sem, fx_sem, b_sem,
):
    incoming = (incoming_0, incoming_1)
    me = lax.axis_index("req")
    seq = lax.axis_index("seq")
    s = seq // 2
    c = seq % 2
    x = me // 4
    y = me % 4
    mate = s * 2 + (1 - c)
    above = lax.rem(s + 1, NZ) * 2 + c
    below = lax.rem(s + NZ - 1, NZ) * 2 + c

    def to(step):
        dx = jnp.where(c == 0, step[0], 4 - step[0])
        dy = jnp.where(c == 0, step[1], 4 - step[1])
        return lax.rem(x + dx, 4) * 4 + lax.rem(y + dy, 4)

    def back(step):
        return to((4 - step[0], 4 - step[1]))

    barrier = pltpu.get_barrier_semaphore()
    for step in ROUTES:
        pl.semaphore_signal(barrier, inc=1, device_id=(to(step), seq), device_id_type=MESH)
    for z in (mate, above, below):
        pl.semaphore_signal(barrier, inc=1, device_id=(me, z), device_id_type=MESH)

    for h in range(16):
        qh[h] = q[:, h * D : (h + 1) * D]

    def build(r, carry):
        count = jnp.int32(0)
        first = jnp.int32(0)
        second = jnp.int32(0)
        for j in range(PIECES):
            hit = owner[r, j] == me
            value = slot[r, j]
            first = jnp.where(hit & (count == 0), value, first)
            second = jnp.where(hit & (count == 1), value, second)
            count = count + hit.astype(jnp.int32)
        for k, at in ((0, first), (1, second)):
            piece = store[at]
            for p in range(2):
                for i in range(4):
                    col = (i % 2) * 512 + ((i // 2) * 2 + p) * D
                    outgoing[p, r, k, :, i * D : (i + 1) * D] = piece[:, col : col + D]
        return carry

    lax.fori_loop(0, NREQ, build, 0)
    pl.semaphore_wait(barrier, NREQ - 1 + 3)

    def direct(p, i, arriving):
        other = back(ROUTES[i]) if arriving else to(ROUTES[i])
        row = other if arriving else me
        return remote(
            outgoing.at[p, other], incoming[p].at[row], a_send.at[p, i], a_recv.at[p, i], other, seq
        )

    def exchange_start(p):
        for i in range(len(ROUTES)):
            direct(p, i, False).start()

    def q_msg(p, h, z, t, up):
        k = 1 if up else 0
        ref = qg.at[z, pl.ds(p * 4 + 2 * h, 2)]
        return remote(
            ref, ref, qs_sem.at[p, h, k, t], qr_sem.at[p, h, k, t], me, above if up else below
        )

    def q_arrive(p, h, t):
        z_down = s + t
        z_up = lax.rem(s - t + NZ, NZ)
        if t < 4 or h == 0:

            @pl.when(z_down <= NZ - 1)
            def _():
                q_msg(p, h, z_down, t, False).wait_recv()

        if t < 4 or h == 1:

            @pl.when(z_up >= 4)
            def _():
                q_msg(p, h, z_up, t, True).wait_recv()

    def q_leave(p, h, t, over):
        z_down = s + t - 1
        z_up = lax.rem(s - t + 1 + NZ, NZ)
        if t < 4 or h == 0:

            @pl.when((z_down <= NZ - 1) & (s >= 1))
            def _():
                m = q_msg(p, h, z_down, t, False)
                m.wait_send() if over else m.start()

        if t < 4 or h == 1:

            @pl.when(z_up >= 4)
            def _():
                m = q_msg(p, h, z_up, t, True)
                m.wait_send() if over else m.start()

    qx = remote(qh.at[pl.ds((1 - c) * 8, 8)], qg.at[s, :, c], qx_sem.at[0], qx_sem.at[1], me, mate)
    qx.start()
    exchange_start(0)
    for h in range(8):
        qg[s, h, c] = qh[c * 8 + h]
    remote(qh.at[pl.ds(0, 8)], qg.at[s, :, 1 - c], qx_sem.at[0], qx_sem.at[1], me, mate).wait_recv()
    for h in range(2):
        q_leave(0, h, 1, False)
    for p in range(2):
        incoming[p][me] = outgoing[p, me]

    eye = lax.broadcasted_iota(jnp.int32, (SEL, D), 0) == lax.broadcasted_iota(jnp.int32, (SEL, D), 1)

    def to_col(row):
        return jnp.sum(jnp.where(eye, row, 0.0), axis=1, keepdims=True)

    def to_row(col):
        return jnp.sum(jnp.where(eye, col, 0.0), axis=0, keepdims=True)

    for t in range(2, 5):
        for h in range(2):
            q_arrive(0, h, t - 1)
            q_leave(0, h, t, False)
    for h in range(2):
        q_leave(1, h, 1, False)
    for h in range(2):
        q_arrive(0, h, 4)

    def gathered(p):
        for i in range(len(ROUTES)):
            direct(p, i, True).wait_recv()
        if p == 0:
            exchange_start(1)
        mine = [owner[me, j] for j in range(PIECES)]
        for j in range(PIECES):
            rank = jnp.int32(0)
            for k in range(j):
                rank = rank + (mine[k] == mine[j]).astype(jnp.int32)
            cached[j * PASSAGE : (j + 1) * PASSAGE, :] = incoming[p][mine[j], jnp.minimum(rank, 1)]

    def blend_in(p):
        own_row = pos[0:1, :]
        index = lax.broadcasted_iota(jnp.int32, (SEL, TOK), 1).astype(F32)
        pick = jnp.where(index == to_col(own_row), 1.0, 0.0).astype(BF16)
        put = jnp.where(lax.broadcasted_iota(jnp.int32, (TOK, D), 0).astype(F32) == own_row, 1.0, 0.0)
        hit_col = jnp.sum(put, axis=1, keepdims=True) > 0.5
        put = put.astype(BF16)[:, :SEL]
        for core in range(2):
            total = None
            for k in range(2):
                cols = pl.ds(pl.multiple_of(k * 512 + (core * 2 + p) * D, D), D)
                old = cached[:, (core * 2 + k) * D : (core * 2 + k + 1) * D]
                new = fresh_kv[:, cols]
                placed = jnp.dot(put, new, preferred_element_type=F32)
                both = jnp.where(hit_col, placed, old.astype(F32)).astype(BF16)
                blend[:, cols] = both
                bh[p, core, k] = both
                diff = new.astype(F32) - jnp.dot(pick, old, preferred_element_type=F32)
                total = diff * diff if total is None else total + diff * diff
            squares[core * 2 + p] = total

    def keys_msg(p, arriving):
        if arriving:
            return remote(bh.at[p, c], kv.at[p, :, 1 - c], kx_send.at[p], kx_recv.at[p], me, mate)
        return remote(bh.at[p, 1 - c], kv.at[p, :, c], kx_send.at[p], kx_recv.at[p], me, mate)

    def attend(zd, p, masked):
        rows = qg[zd, pl.ds(p * 4, 4)].reshape(8 * SEL, D)
        if masked:
            limit = [to_col(pos[1:2, :]), to_col(pos[2:3, :])]
            limit = jnp.concatenate(limit * 4, axis=0)
        top = total = product = None
        for i in range(CHIP_TOK // CHUNK):
            at = i * CHUNK
            keys = [kv[p, 0].reshape(CHIP_TOK, D)[at : at + CHUNK], kv[p, 1].reshape(CHIP_TOK, D)[at : at + CHUNK]]
            scores = lax.dot_general(
                rows, keys[0], (((1,), (1,)), ((), ())), preferred_element_type=F32
            )
            if masked:
                index = lax.broadcasted_iota(jnp.int32, (8 * SEL, CHUNK), 1).astype(F32) + float(at)
                scores = jnp.where(index <= limit, scores, EMPTY)
            high = jnp.max(scores, axis=1, keepdims=True)
            if top is not None:
                high = jnp.maximum(top, high)
            weights = jnp.exp2((scores - high) * C2)
            sums = weights[:, :D] + weights[:, D:]
            now = jnp.dot(weights.astype(BF16), keys[1], preferred_element_type=F32)
            if top is None:
                total, product = sums, now
            else:
                shrink = jnp.exp2((top - high) * C2)
                total = total * shrink + sums
                product = product * shrink + now
            top = high
        total = jnp.sum(total, axis=1, keepdims=True)
        part[zd, pl.ds(p * 4, 4)] = (product / total).astype(BF16).reshape(4, 2, SEL, D)
        level = top * C2 + jnp.log2(total)
        for g in range(8):
            lse[zd, p, g // 4, g % 4 : g % 4 + 1, :] = to_row(level[g * SEL : (g + 1) * SEL])

    def merge(zd, p, k, at, h):
        have = lse[zd, p, h]
        came = buf_l[k, at, p, h]
        high = jnp.maximum(have, came)
        e_have = jnp.exp2(have - high)
        e_came = jnp.exp2(came - high)
        total = e_have + e_came
        part_of = e_came / total
        lse[zd, p, h] = high + jnp.log2(total)
        for g in range(2):
            for b in range(2):
                w = to_col(part_of[g * 2 + b : g * 2 + b + 1, :])
                a = part[zd, p * 4 + h * 2 + g, b].astype(F32)
                n = buf_o[k, at, p * 4 + h * 2 + g, b].astype(F32)
                part[zd, p * 4 + h * 2 + g, b] = (a + w * (n - a)).astype(BF16)

    def p_msgs(zd, p, d, k, h, peer):
        heads = pl.ds(p * 4 + h * 2, 2)
        return (
            remote(
                part.at[zd, heads], buf_o.at[k, d - 1, heads],
                ps_sem.at[p, k, d, h, 0], pr_sem.at[p, k, d - 1, h, 0], me, peer,
            ),
            remote(
                lse.at[zd, p, h], buf_l.at[k, d - 1, p, h],
                ps_sem.at[p, k, d, h, 1], pr_sem.at[p, k, d - 1, h, 1], me, peer,
            ),
        )

    far = lax.rem(s + 4, NZ)

    def phase(p, whole):
        for n in range(2):

            @pl.when(p == n)
            def _(n=n):
                gathered(n)

        blend_in(p)
        keys_msg(p, False).start()
        for k in range(2):
            kv[p, k, c] = bh[p, c, k]

        @pl.when(p == 1)
        def _():
            for h in range(2):
                q_arrive(1, h, 4)

        keys_msg(p, True).wait_recv()

        @pl.when(s <= 3)
        def _():
            attend(far, p, False)
            for k, peer in ((0, above), (1, below)):
                for m in p_msgs(far, p, 4, k, k, peer):
                    m.start()

        def ring(i, carry):
            d = 3 - i // 2
            k = lax.rem(i, 2)
            up = k == 0
            zd = jnp.where(up, lax.rem(s + d, NZ), lax.rem(s - d + NZ, NZ))
            peer = jnp.where(up, above, below)
            active = jnp.where(up, s + d, jnp.where(zd >= 4, 0, NZ)) <= NZ - 1
            comes = active & ((k == 1) | (s >= 1))

            for n in range(3):

                @pl.when((p == 0) & (i == 2 * n))
                def _(n=n):
                    for h in range(2):
                        q_arrive(1, h, n + 1)
                        q_leave(1, h, n + 2, False)

            @pl.when(active & (zd > s))
            def _():
                attend(zd, p, False)

            @pl.when(active & (zd < s))
            def _():
                part[zd, pl.ds(p * 4, 4)] = jnp.zeros((4, 2, SEL, D), BF16)
                lse[zd, p] = jnp.full((2, 4, D), EMPTY, F32)

            def pass_on(h, inner):
                @pl.when(comes & ((d < 3) | (h == k)))
                def _():
                    for m in p_msgs(zd, p, d + 1, k, h, peer):
                        m.wait_recv()
                    merge(zd, p, k, d, h)

                @pl.when(active)
                def _():
                    for m in p_msgs(zd, p, d, k, h, peer):
                        m.start()

                return inner

            lax.fori_loop(0, 2, pass_on, 0)
            return carry

        @pl.when(s >= 4)
        def _():
            attend(s, p, True)

        lax.fori_loop(0, 6, ring, 0)

        @pl.when(s < 4)
        def _():
            attend(s, p, True)

        return whole

    lax.fori_loop(0, 2, phase, 0)
    out_copy = pltpu.make_async_copy(blend, blended_out, b_sem)
    out_copy.start()
    for h in range(4):
        dev[h : h + 1, :] = to_row(jnp.sum(squares[h], axis=1, keepdims=True))[:, :SEL]

    def finish(p, carry):
        for k, cond in ((0, s >= 1), (1, s >= 4)):

            @pl.when(cond)
            def _(k=k):
                for h in range(2):
                    for m in p_msgs(s, p, 1, k, h, below):
                        m.wait_recv()
                    merge(s, p, k, 0, h)

        return carry

    lax.fori_loop(0, 2, finish, 0)
    fx = remote(part.at[s, :, 1 - c], fin.at[pl.ds(c * 8, 8)], fx_sem.at[0], fx_sem.at[1], me, mate)
    fx.start()
    for h in range(8):
        fin[c * 8 + h] = part[s, h, c]

    def drain(p, carry):
        keys_msg(p, False).wait_send()
        for t in range(1, 5):
            for h in range(2):
                q_leave(p, h, t, True)

        @pl.when(s <= 3)
        def _():
            for k, peer in ((0, above), (1, below)):
                for m in p_msgs(far, p, 4, k, k, peer):
                    m.wait_send()

        def sent(i, inner):
            d = 3 - i // 2
            k = lax.rem(i, 2)
            up = k == 0
            zd = jnp.where(up, lax.rem(s + d, NZ), lax.rem(s - d + NZ, NZ))
            active = jnp.where(up, s + d, jnp.where(zd >= 4, 0, NZ)) <= NZ - 1

            @pl.when(active)
            def _():
                for h in range(2):
                    for m in p_msgs(zd, p, d, k, h, above):
                        m.wait_send()

            return inner

        lax.fori_loop(0, 6, sent, 0)
        return carry

    lax.fori_loop(0, 2, drain, 0)
    for p in range(2):
        for i in range(len(ROUTES)):
            direct(p, i, False).wait_send()
    qx.wait_send()
    remote(
        part.at[s, :, c], fin.at[pl.ds((1 - c) * 8, 8)], fx_sem.at[0], fx_sem.at[1], me, mate
    ).wait_recv()
    for h in range(16):
        att[:, h * D : (h + 1) * D] = fin[h]
    fx.wait_send()
    out_copy.wait()


def hand_on(a_in, b_in, c_in, a_out, b_out, c_out, a_mid, b_mid, c_mid, sem_in, sem_out):
    ways = [(c_in, c_mid, c_out), (b_in, b_mid, b_out)]
    for i in range(4):
        rows = pl.ds(i * (TOK // 4), TOK // 4)
        ways.append((a_in.at[rows], a_mid.at[rows], a_out.at[rows]))
    taken = [pltpu.make_async_copy(w[0], w[1], sem_in.at[i]) for i, w in enumerate(ways)]
    given = [pltpu.make_async_copy(w[1], w[2], sem_out.at[i]) for i, w in enumerate(ways)]
    for copy in taken:
        copy.start()
    for first, then in zip(taken, given):
        first.wait()
        then.start()
    for copy in given:
        copy.wait()


def body(store, passage_owner, passage_slot, sel_pos, queries, new_kv):
    seq = lax.axis_index("seq")
    chip = seq // 2
    core = seq % 2
    owner = passage_owner[:, :, 0]
    near = lax.dynamic_slice(sel_pos[0], (chip * 2 * SEL,), (2 * SEL,)).reshape(2, SEL) - chip * CHIP_TOK
    own = lax.dynamic_index_in_dim(near, core, 0, keepdims=True) - core * TOK
    pos = jnp.concatenate([own, near], axis=0)
    pos = jnp.pad(pos, ((0, 5), (0, D - SEL)), constant_values=-1).astype(F32)
    vmem = pl.BlockSpec(memory_space=pltpu.VMEM)
    smem = pl.BlockSpec(memory_space=pltpu.SMEM)
    dma = pltpu.SemaphoreType.DMA
    blended, deviation, attended = pl.pallas_call(
        kernel,
        out_shape=(
            jax.ShapeDtypeStruct((TOK, KVW), BF16),
            jax.ShapeDtypeStruct((4, SEL), F32),
            jax.ShapeDtypeStruct((SEL, QW), BF16),
        ),
        in_specs=[smem, smem, vmem, vmem, vmem, vmem],
        out_specs=(pl.BlockSpec(memory_space=pl.ANY), vmem, vmem),
        scratch_shapes=[
            pltpu.VMEM((2, NREQ, 2, PASSAGE, KVW // 2), BF16),
            pltpu.VMEM((NREQ, 2, PASSAGE, KVW // 2), BF16),
            pltpu.VMEM((NREQ, 2, PASSAGE, KVW // 2), BF16),
            pltpu.VMEM((16, SEL, D), BF16),
            pltpu.VMEM((NZ, 8, 2, SEL, D), BF16),
            pltpu.VMEM((TOK, KVW // 2), BF16),
            pltpu.VMEM((TOK, KVW), BF16),
            pltpu.VMEM((2, 2, 2, TOK, D), BF16),
            pltpu.VMEM((2, 2, 2, TOK, D), BF16),
            pltpu.VMEM((NZ, 8, 2, SEL, D), BF16),
            pltpu.VMEM((NZ, 2, 2, 4, D), F32),
            pltpu.VMEM((2, 4, 8, 2, SEL, D), BF16),
            pltpu.VMEM((2, 4, 2, 2, 4, D), F32),
            pltpu.VMEM((16, SEL, D), BF16),
            pltpu.VMEM((4, SEL, D), F32),
            dma((2, len(ROUTES))),
            dma((2, len(ROUTES))),
            dma((2,)),
            dma((2, 2, 2, 5)),
            dma((2, 2, 2, 5)),
            dma((2,)),
            dma((2,)),
            dma((2, 2, 5, 2, 2)),
            dma((2, 2, 5, 2, 2)),
            dma((2,)),
            dma,
        ],
        compiler_params=pltpu.CompilerParams(
            collective_id=0, has_side_effects=True, vmem_limit_bytes=60 * 1024 * 1024,
        ),
    )(owner, passage_slot, pos, store[:, 0], queries[0], new_kv[0])
    blended, deviation, attended = pl.pallas_call(
        hand_on,
        out_shape=(
            jax.ShapeDtypeStruct((TOK, KVW), BF16),
            jax.ShapeDtypeStruct((4, SEL), F32),
            jax.ShapeDtypeStruct((SEL, QW), BF16),
        ),
        in_specs=[pl.BlockSpec(memory_space=pl.ANY)] * 3,
        out_specs=(pl.BlockSpec(memory_space=pl.ANY),) * 3,
        scratch_shapes=[
            pltpu.VMEM((TOK, KVW), BF16),
            pltpu.VMEM((4, SEL), F32),
            pltpu.VMEM((SEL, QW), BF16),
            dma((6,)),
            dma((6,)),
        ],
    )(blended, deviation, attended)
    return blended[None], deviation.T[None], attended[None]


def solution(mesh):
    placed = (
        P("req", "seq", None, None),
        P(None, "seq", None),
        P(None, "seq"),
        P("req", None),
        P("req", "seq", None),
        P("req", "seq", None),
    )
    return jax.shard_map(
        body,
        mesh=mesh,
        in_specs=placed,
        out_specs=(P("req", "seq", None), P("req", "seq", None), P("req", "seq", None)),
        check_vma=False,
    )
```
